32 devices in a mesh: groups: 2 (over y), blk: 4 (over z), rep: 4 (over x, core).
Axes of the slice: x: 2, y: 2, z: 4, core: 2. Of those that a mesh axis runs over, the one named last changes fastest.
Arguments:
- embeddings: float32 [8192, 128], P(('groups', 'blk')), parts along dimension 0, may hold values from -6 to 6
- degrees: int32 [8192], P(('groups', 'blk')), parts along dimension 0, may hold values from 1 to 12800, as said below
- tile_values: bfloat16 [8, 4, 1, 24, 128, 128], P(('groups', 'blk'), 'rep'), parts along dimension 0
- tile_rows: int32 [8, 4, 1, 24], P(('groups', 'blk'), 'rep'), parts along dimension 0, may hold values from 0 to 7
- tile_columns: int32 [8, 4, 1, 24], P(('groups', 'blk'), 'rep'), parts along dimension 0, may hold values from 0 to 7
- slot_counts: int32 [8, 4, 1], P(('groups', 'blk'), 'rep'), parts along dimension 0, may hold values from 6 to 24, as said below
Outputs:
- combined: float32 [8192, 128], P(('groups', 'blk', 'rep')), parts along dimension 0
The draws below stay inside these ranges and needn't reach their ends.
There are 2 independent parts, one for each index of `groups`. The reference program is written for one: setup_inputs(seed, part) draws one part's arguments, and reference() takes and returns one part's arrays. A program takes and returns all parts, laid end to end along the dimension named above; each array names one. Nothing has to cross between parts.
Inputs may be any that keep to these rules, and one draw needn't show every extreme that they name: `degrees`: each node's degree is at least the number of nonzero entries in its row of A. `slot_counts`: some arc position of some device has all 24 slots live in every draw.
All inputs are finite; a program needn't handle non-finite values.
Results may differ from the reference program's by a relative error of at most 0.0003.
Values sent between devices are 32-bit elements; how exact they have to be, the bound alone decides.
A program may use at most 64 MiB of HBM per device.

```python
import math
import jax
import jax.numpy as jnp
from jax import lax

WIDTH = 128
TILE = 128
RB_DEV = 8
CAP = 24
LAYERS = 2
CYCLE = 4
TEAMS = 4
ARC = 1
NODES = 4096


def shard_keys(key, shard_index):
    own_key = jax.random.fold_in(key, 202)
    shard_key = jax.random.fold_in(own_key, shard_index)
    return jax.random.split(shard_key)


def shard_mask(key, shard_index):
    mask_key, value_key = shard_keys(key, shard_index)
    slot_shape = (TEAMS, ARC, CAP, TILE, TILE)
    return jax.random.randint(mask_key, slot_shape, 0, 4) == 0


def rows_helper(key):
    own_key = jax.random.fold_in(key, 303)
    first_key, second_key = jax.random.split(own_key)
    slot_shape = (CYCLE, TEAMS, ARC, CAP)
    first_rows = jax.random.randint(first_key, slot_shape, 0, RB_DEV)
    second_rows = jax.random.randint(second_key, slot_shape, 0, RB_DEV)
    return jnp.minimum(first_rows, second_rows).astype(jnp.int32)


def counts_helper(key):
    own_key = jax.random.fold_in(key, 404)
    halve_key, chosen_key = jax.random.split(own_key)
    count_shape = (CYCLE, TEAMS, ARC)
    halvings = jax.random.randint(halve_key, count_shape, 0, 3)
    full_value = jnp.full(count_shape, CAP, jnp.int32)
    counts = jnp.maximum(jnp.right_shift(full_value, halvings), 1)
    flat_counts = counts.reshape(-1)
    chosen_slot = jax.random.randint(chosen_key, (), 0, CYCLE * TEAMS * ARC)
    flat_counts = jnp.where(jnp.arange(CYCLE * TEAMS * ARC) == chosen_slot, CAP, flat_counts)
    return flat_counts.reshape(count_shape).astype(jnp.int32)


def draw_degrees(key, part):
    own_key = jax.random.fold_in(key, 101)
    power_key, extra_key, top_key = jax.random.split(own_key, 3)
    exponents = jax.random.randint(power_key, (NODES,), 0, 9)
    base_value = jnp.left_shift(jnp.ones((NODES,), jnp.int32), exponents)
    extra_value = jax.random.randint(extra_key, (NODES,), 0, base_value)
    outside = base_value + extra_value
    all_rows = rows_helper(key)
    all_counts = counts_helper(key)
    slot_numbers = jnp.arange(CAP, dtype=jnp.int32)
    block_numbers = jnp.arange(RB_DEV, dtype=jnp.int32)

    def one_shard(shard_index):
        kept = shard_mask(key, shard_index).astype(jnp.int32)
        live = (slot_numbers < all_counts[shard_index][..., None]).astype(jnp.int32)
        row_nonzeros = jnp.sum(kept, axis=-1) * live[..., None]
        onehot = (all_rows[shard_index][..., None] == block_numbers).astype(jnp.int32)
        return jnp.einsum('rkjc,rkja->ca', onehot, row_nonzeros)
    inside = lax.map(one_shard, jnp.arange(CYCLE, dtype=jnp.int32)).reshape(NODES)
    total = (inside + outside).astype(jnp.int32)
    top_node = jax.random.randint(top_key, (), 0, NODES)
    top_value = CYCLE * CAP * TILE + 512
    return jnp.where(jnp.arange(NODES, dtype=jnp.int32) == top_node, top_value, total).astype(jnp.int32)


def draw_tile_values(key, part):
    slot_shape = (TEAMS, ARC, CAP, TILE, TILE)

    def one_shard(shard_index):
        mask_key, value_key = shard_keys(key, shard_index)
        kept_mask = shard_mask(key, shard_index)
        weights = jnp.exp(jax.random.uniform(value_key, slot_shape, jnp.float32, math.log(0.5), math.log(5.0)))
        return jnp.where(kept_mask, weights, 0.0).astype(jnp.bfloat16)
    return lax.map(one_shard, jnp.arange(CYCLE, dtype=jnp.int32))


def draw_tile_rows(key, part):
    return rows_helper(key)


def draw_slot_counts(key, part):
    return counts_helper(key)


def plant(values, stream_key, smallest, largest):
    place = [jax.random.randint(jax.random.fold_in(stream_key, axis), (), 0, length) for axis, length in enumerate(values.shape)]
    widest = values.shape.index(max(values.shape))
    next_to = place[:widest] + [(place[widest] + 1) % values.shape[widest]] + place[widest + 1:]
    return values.at[tuple(place)].set(smallest).at[tuple(next_to)].set(largest)


def level_of(rng, shape, pieces, low, largest):
    factor_of = 1.0
    for dim, shards_of in pieces:
        draws = jax.random.uniform(jax.random.fold_in(jax.random.fold_in(rng, 6), dim), (shards_of,), jnp.float32, low / len(pieces), largest / len(pieces))
        factor_of = factor_of * jnp.repeat(jnp.exp(draws), shape[dim] // shards_of).reshape((-1,) + (1,) * (len(shape) - 1 - dim))
    return factor_of


def scatter_about(key, shape, scale, reach, pieces=(), held_as=jnp.bfloat16):
    entries = jax.random.normal(key, shape, jnp.float32) * scale
    if len(pieces) > 0:
        entries = level_of(key, shape, pieces, -0.22, 0.18) * entries
    return jnp.clip(entries, min=-reach, max=reach).astype(held_as)


def setup_inputs(seed: int = 0, part: int = 0) -> dict:
    arg_keys = jax.random.split(jax.random.key(seed), 7)
    part_splits = jax.random.split(jax.random.fold_in(arg_keys[6], part), 7)
    embeddings = scatter_about(part_splits[0], (NODES, WIDTH), 1.0, 6.0, ((0, 4),), jnp.float32)
    degrees = draw_degrees(jax.random.fold_in(jax.random.fold_in(arg_keys[6], part), 71), part)
    tile_values = draw_tile_values(jax.random.fold_in(jax.random.fold_in(arg_keys[6], part), 71), part)
    tile_rows = draw_tile_rows(jax.random.fold_in(jax.random.fold_in(arg_keys[6], part), 71), part)
    tile_columns = plant(jax.random.randint(part_splits[4], (CYCLE, TEAMS, ARC, CAP), 0, RB_DEV), jax.random.fold_in(part_splits[4], 1), 0, RB_DEV - 1).astype(jnp.int32)
    slot_counts = draw_slot_counts(jax.random.fold_in(jax.random.fold_in(arg_keys[6], part), 71), part)
    return {"embeddings": embeddings, "degrees": degrees, "tile_values": tile_values, "tile_rows": tile_rows, "tile_columns": tile_columns, "slot_counts": slot_counts}


def propagate(current, norm_scale, tile_values, tile_rows, tile_columns, slot_counts):
    scaled = (current * norm_scale[:, None]).reshape(CYCLE, RB_DEV, TILE, WIDTH)
    team_offsets = jnp.arange(TEAMS, dtype=jnp.int32)[:, None] * ARC
    arc_offsets = jnp.arange(ARC, dtype=jnp.int32)[None, :]
    slot_numbers = jnp.arange(CAP, dtype=jnp.int32)
    block_numbers = jnp.arange(RB_DEV, dtype=jnp.int32)

    def shard_rows(shard_index):
        sources = jnp.mod(shard_index - team_offsets - arc_offsets, CYCLE).astype(jnp.int32)
        columns = tile_columns[shard_index]
        blocks = scaled[sources[:, :, None], columns]
        products = jnp.einsum('rkjab,rkjbw->rkjaw', tile_values[shard_index].astype(jnp.float32), blocks, precision=lax.Precision.HIGHEST)
        live_slots = slot_numbers < slot_counts[shard_index][..., None]
        placement = ((tile_rows[shard_index][..., None] == block_numbers) & live_slots[..., None]).astype(jnp.float32)
        return jnp.einsum('rkjc,rkjaw->caw', placement, products, precision=lax.Precision.HIGHEST)
    summed = lax.map(shard_rows, jnp.arange(CYCLE, dtype=jnp.int32))
    return summed.reshape(NODES, WIDTH) * norm_scale[:, None]

def reference(embeddings, degrees, tile_values, tile_rows, tile_columns, slot_counts):
    norm_scale = lax.rsqrt(degrees.astype(jnp.float32))
    current = embeddings
    combined = embeddings
    for layer_index in range(LAYERS):
        current = propagate(current, norm_scale, tile_values, tile_rows, tile_columns, slot_counts)
        combined = combined + current
    return combined / (LAYERS + 1.0)
```

```python
import functools

import jax
import jax.numpy as jnp
from jax import lax
from jax.experimental import pallas as pl
from jax.experimental.pallas import tpu as pltpu
from jax.sharding import PartitionSpec as P

LAYERS = 2
MESH = pl.DeviceIdType.MESH


def shifted_2(shard, axis, by):
    devices = lax.axis_size(axis)
    return lax.ppermute(shard, axis, [(i, (i + by) % devices) for i in range(devices)])


def slot_term(source_panel, arc_slot, slots):
    tile_values, tile_rows, tile_columns, slot_counts = slots
    slot_total = tile_values.shape[1]
    block_total = source_panel.shape[0]
    columns = lax.dynamic_index_in_dim(tile_columns, arc_slot, 0, keepdims=False)
    values = lax.dynamic_index_in_dim(tile_values, arc_slot, 0, keepdims=False)
    row_blocks = lax.dynamic_index_in_dim(tile_rows, arc_slot, 0, keepdims=False)
    live_count = lax.dynamic_index_in_dim(slot_counts, arc_slot, 0, keepdims=False)
    blocks = jnp.take(source_panel, columns, axis=0)
    products = jnp.einsum(
        "jab,jbw->jaw",
        values,
        blocks,
        precision=lax.Precision.HIGHEST,
        preferred_element_type=jnp.float32,
    )
    live_slots = jnp.arange(slot_total, dtype=jnp.int32) < live_count
    placement = (
        (row_blocks[:, None] == jnp.arange(block_total, dtype=jnp.int32)[None, :])
        & live_slots[:, None]
    ).astype(jnp.float32)
    return jnp.einsum("jc,jaw->caw", placement, products, precision=lax.Precision.HIGHEST)


def arc_product(source_panel, slots, team_index, team_count):
    arc_length = slots[0].shape[0]
    arc_panel = source_panel
    for power_index in range(team_count.bit_length() - 1):
        shifted = shifted_2(arc_panel, "blk", arc_length * (1 << power_index))
        arc_panel = jnp.where(team_index >> power_index & 1 == 1, shifted, arc_panel)
    empty = jnp.zeros(source_panel.shape, jnp.float32)

    def walk(arc_slot, loop_state):
        partial_value, panel_now = loop_state
        partial_value = partial_value + slot_term(panel_now, arc_slot, slots)
        panel_now = shifted_2(panel_now, "blk", 1)
        return (partial_value, panel_now)

    partial_value, panel_now = lax.fori_loop(0, arc_length - 1, walk, (empty, arc_panel))
    return partial_value + slot_term(panel_now, arc_length - 1, slots)


def per_device(embeddings, degrees, tile_values, tile_rows, tile_columns, slot_counts):
    tile_size = tile_values.shape[-1]
    width_count = embeddings.shape[1]
    block_count = embeddings.shape[0] // tile_size
    slots = (tile_values[0, 0], tile_rows[0, 0], tile_columns[0, 0], slot_counts[0, 0])
    team_index = lax.axis_index("rep")
    team_count = lax.axis_size("rep")
    share_rows = embeddings.shape[0] // team_count
    norm_scale = lax.rsqrt(degrees.astype(jnp.float32))
    current = embeddings
    combined = lax.dynamic_slice_in_dim(embeddings, team_index * share_rows, share_rows)
    for layer_index in range(LAYERS):
        source_panel = (current * norm_scale[:, None]).reshape(block_count, tile_size, width_count)
        partial_value = arc_product(source_panel, slots, team_index, team_count)
        partial_value = partial_value.reshape(block_count * tile_size, width_count)
        current = lax.psum(partial_value, "rep") * norm_scale[:, None]
        combined = combined + lax.dynamic_slice_in_dim(current, team_index * share_rows, share_rows)
    return combined / (LAYERS + 1.0)


def team_kernel(
    teams, emb_hbm, deg_ref, tiles_hbm, rows_ref, cols_ref, counts_ref, out_ref,
    emb_own, norm_own, tiles, running, running_hi, running_lo, keys, a_hi, a_lo,
    x_send, x_recv, x_pair, p_send, p_recv,
    local_sems, x_send_sems, x_recv_sems, p_send_sems, p_recv_sems,
):
    z = lax.axis_index("blk")
    r = lax.axis_index("rep")
    slots, tile_size, width = tiles.shape[0], tiles.shape[1], emb_own.shape[1]
    share = emb_own.shape[0]
    side = a_hi.shape[0] // tile_size
    blocks_own = share // tile_size

    load_emb = pltpu.make_async_copy(
        emb_hbm.at[pl.ds(pl.multiple_of(r * share, share), share)], emb_own, local_sems.at[0]
    )
    load_tiles = pltpu.make_async_copy(tiles_hbm, tiles, local_sems.at[1])
    load_emb.start()
    load_tiles.start()

    barrier = pltpu.get_barrier_semaphore()
    for dz in range(teams):
        for dr in range(teams):
            if dz or dr:
                pl.semaphore_signal(
                    barrier,
                    inc=1,
                    device_id={"blk": lax.rem(z + dz, teams), "rep": lax.rem(r + dr, teams)},
                    device_id_type=MESH,
                )

    for i in range(blocks_own):
        scale_row = lax.rsqrt(deg_ref[r * blocks_own + i].astype(jnp.float32))
        norm_own[i * tile_size : (i + 1) * tile_size] = jnp.broadcast_to(
            scale_row, (width, tile_size)
        ).T
    load_emb.wait()
    x_send[0] = emb_own[...] * norm_own[...]
    pl.semaphore_wait(barrier, teams * teams - 1)

    def x_copy(layer, team):
        return pltpu.make_async_remote_copy(
            src_ref=x_send.at[layer],
            dst_ref=x_recv.at[layer, r],
            send_sem=x_send_sems.at[layer, team],
            recv_sem=x_recv_sems.at[layer, r],
            device_id={"blk": lax.rem(z + team, teams), "rep": team},
            device_id_type=MESH,
        )

    def x_arrival(layer, quarter):
        return pltpu.make_async_remote_copy(
            src_ref=x_send.at[layer],
            dst_ref=x_recv.at[layer, quarter],
            send_sem=x_send_sems.at[layer, quarter],
            recv_sem=x_recv_sems.at[layer, quarter],
            device_id={"blk": lax.rem(z + 1, teams), "rep": r},
            device_id_type=MESH,
        )

    def send_x(layer):
        for team in (2, 3, 1):
            x_copy(layer, team).start()

        @pl.when(r != 0)
        def _():
            x_copy(layer, 0).start()

        @pl.when(r == 0)
        def _():
            x_recv[layer, 0] = x_send[layer]

    def take_x(layer):
        for quarter in (1, 2, 3, 0):
            if quarter == 0:
                @pl.when(r != 0)
                def _():
                    x_arrival(layer, 0).wait_recv()
            else:
                x_arrival(layer, quarter).wait_recv()
            value = x_recv[layer, quarter]
            high = value.astype(jnp.bfloat16)
            low = (value - high.astype(jnp.float32)).astype(jnp.bfloat16)
            x_pair[quarter * share : (quarter + 1) * share, :width] = high
            x_pair[quarter * share : (quarter + 1) * share, width:] = low

    def build():
        live = counts_ref[0]
        for j in range(slots):
            keys[j] = jnp.where(j < live, rows_ref[j] * side + cols_ref[j], side * side)
        running[0] = jnp.zeros((tile_size, tile_size), jnp.float32)
        running_hi[0] = jnp.zeros((tile_size, tile_size), jnp.bfloat16)
        running_lo[0] = jnp.zeros((tile_size, tile_size), jnp.bfloat16)
        load_tiles.wait()

        def accumulate(j, carry):
            own_key = keys[j]
            before = jnp.int32(0)
            for i in range(slots):
                before = jnp.where((keys[i] == own_key) & (i < j), i + 1, before)
            total = running[before] + tiles[j].astype(jnp.float32)
            high = total.astype(jnp.bfloat16)
            running[j + 1] = total
            running_hi[j + 1] = high
            running_lo[j + 1] = (total - high.astype(jnp.float32)).astype(jnp.bfloat16)
            return carry

        lax.fori_loop(0, slots, accumulate, 0)

        def place(row, carry):
            start = pl.multiple_of(row * tile_size, tile_size)
            for column in range(side):
                last = jnp.int32(0)
                for j in range(slots):
                    last = jnp.where(keys[j] == row * side + column, j + 1, last)
                span = slice(column * tile_size, (column + 1) * tile_size)
                a_hi[pl.ds(start, tile_size), span] = running_hi[last]
                a_lo[pl.ds(start, tile_size), span] = running_lo[last]
            return carry

        lax.fori_loop(0, side, place, 0)

    def product(part):
        start = pl.multiple_of(part * share, share)
        both = jnp.dot(
            a_hi[pl.ds(start, share), :], x_pair[...], preferred_element_type=jnp.float32
        )
        rest = jnp.dot(
            a_lo[pl.ds(start, share), :], x_pair[:, :width], preferred_element_type=jnp.float32
        )
        return both[:, :width] + (both[:, width:] + rest)

    chip, core = r // 2, r % 2
    partners = (2 * (1 - chip) + core, 2 * (1 - chip) + (1 - core), 2 * chip + (1 - core))

    def p_copy(layer, turn):
        return pltpu.make_async_remote_copy(
            src_ref=p_send.at[layer, turn],
            dst_ref=p_recv.at[layer, turn],
            send_sem=p_send_sems.at[layer, turn],
            recv_sem=p_recv_sems.at[layer, turn],
            device_id={"blk": z, "rep": partners[turn]},
            device_id_type=MESH,
        )

    send_x(0)
    build()
    combined = None
    for layer in range(LAYERS):
        take_x(layer)
        for turn in range(teams - 1):
            p_send[layer, turn] = product(partners[turn])
            p_copy(layer, turn).start()
        total = product(r)
        for turn in (2, 0, 1):
            p_copy(layer, turn).wait_recv()
            total = total + p_recv[layer, turn]
        current = total * norm_own[...]
        if layer < LAYERS - 1:
            x_send[layer + 1] = current * norm_own[...]
            send_x(layer + 1)
        if layer == 0:
            emb_own[...] = emb_own[...] + current
        else:
            out_ref[...] = (emb_own[...] + current) / (LAYERS + 1.0)

    for layer in range(LAYERS):
        for team in range(1, teams):
            x_copy(layer, team).wait_send()

        @pl.when(r != 0)
        def _():
            x_copy(layer, 0).wait_send()

        for turn in range(teams - 1):
            p_copy(layer, turn).wait_send()


def per_device_fused(embeddings, degrees, tile_values, tile_rows, tile_columns, slot_counts):
    teams = lax.axis_size("rep")
    slots, tile_size = tile_values.shape[3], tile_values.shape[-1]
    nodes, width = embeddings.shape
    share = nodes // teams
    f32, bf16 = jnp.float32, jnp.bfloat16
    smem = pl.BlockSpec(memory_space=pltpu.SMEM)
    vmem = pl.BlockSpec(memory_space=pltpu.VMEM)
    hbm = pl.BlockSpec(memory_space=pl.ANY)
    dma = pltpu.SemaphoreType.DMA
    return pl.pallas_call(
        functools.partial(team_kernel, teams),
        name="team_propagate",
        out_shape=jax.ShapeDtypeStruct((share, width), f32),
        in_specs=[hbm, vmem, hbm, smem, smem, smem],
        out_specs=vmem,
        scratch_shapes=[
            pltpu.VMEM((share, width), f32),
            pltpu.VMEM((share, width), f32),
            pltpu.VMEM((slots, tile_size, tile_size), bf16),
            pltpu.VMEM((slots + 1, tile_size, tile_size), f32),
            pltpu.VMEM((slots + 1, tile_size, tile_size), bf16),
            pltpu.VMEM((slots + 1, tile_size, tile_size), bf16),
            pltpu.SMEM((slots,), jnp.int32),
            pltpu.VMEM((nodes, nodes), bf16),
            pltpu.VMEM((nodes, nodes), bf16),
            pltpu.VMEM((LAYERS, share, width), f32),
            pltpu.VMEM((LAYERS, teams, share, width), f32),
            pltpu.VMEM((nodes, 2 * width), bf16),
            pltpu.VMEM((LAYERS, teams - 1, share, width), f32),
            pltpu.VMEM((LAYERS, teams - 1, share, width), f32),
            dma((2,)),
            dma((LAYERS, teams)),
            dma((LAYERS, teams)),
            dma((LAYERS, teams - 1)),
            dma((LAYERS, teams - 1)),
        ],
        compiler_params=pltpu.CompilerParams(
            collective_id=0, has_side_effects=True, vmem_limit_bytes=40 * 1024 * 1024
        ),
    )(
        embeddings,
        degrees.reshape(nodes // tile_size, 1, tile_size),
        tile_values.reshape(slots, tile_size, tile_size),
        tile_rows.reshape(slots),
        tile_columns.reshape(slots),
        slot_counts.reshape(1),
    )


def program_for(mesh):
    teams, cycle = mesh.shape["rep"], mesh.shape["blk"]

    def run(embeddings, degrees, tile_values, tile_rows, tile_columns, slot_counts):
        nodes, tile_size = embeddings.shape[0], tile_values.shape[-1]
        fits = (
            teams == 4
            and cycle == 4
            and tile_values.shape[2] == 1
            and nodes % (teams * tile_size) == 0
            and nodes <= 1024
            and embeddings.shape[1] == tile_size == 128
        )
        form = per_device_fused if fits else per_device
        return form(embeddings, degrees, tile_values, tile_rows, tile_columns, slot_counts)

    return run


def solution(mesh):
    in_specs = (
        P(("groups", "blk"), None),
        P(("groups", "blk")),
        P(("groups", "blk"), "rep", None, None, None, None),
        P(("groups", "blk"), "rep", None, None),
        P(("groups", "blk"), "rep", None, None),
        P(("groups", "blk"), "rep", None),
    )
    out_specs = P(("groups", "blk", "rep"), None)
    return jax.shard_map(
        program_for(mesh), mesh=mesh, in_specs=in_specs, out_specs=out_specs, check_vma=False
    )
```

```python
import functools

import jax
import jax.numpy as jnp
from jax import lax
from jax.experimental import pallas as pl
from jax.experimental.pallas import tpu as pltpu
from jax.sharding import PartitionSpec as P

LAYERS = 2
MESH = pl.DeviceIdType.MESH


def shifted_2(shard, axis, by):
    devices = lax.axis_size(axis)
    return lax.ppermute(shard, axis, [(i, (i + by) % devices) for i in range(devices)])


def slot_term(source_panel, arc_slot, slots):
    tile_values, tile_rows, tile_columns, slot_counts = slots
    slot_total = tile_values.shape[1]
    block_total = source_panel.shape[0]
    columns = lax.dynamic_index_in_dim(tile_columns, arc_slot, 0, keepdims=False)
    values = lax.dynamic_index_in_dim(tile_values, arc_slot, 0, keepdims=False)
    row_blocks = lax.dynamic_index_in_dim(tile_rows, arc_slot, 0, keepdims=False)
    live_count = lax.dynamic_index_in_dim(slot_counts, arc_slot, 0, keepdims=False)
    blocks = jnp.take(source_panel, columns, axis=0)
    products = jnp.einsum(
        "jab,jbw->jaw",
        values,
        blocks,
        precision=lax.Precision.HIGHEST,
        preferred_element_type=jnp.float32,
    )
    live_slots = jnp.arange(slot_total, dtype=jnp.int32) < live_count
    placement = (
        (row_blocks[:, None] == jnp.arange(block_total, dtype=jnp.int32)[None, :])
        & live_slots[:, None]
    ).astype(jnp.float32)
    return jnp.einsum("jc,jaw->caw", placement, products, precision=lax.Precision.HIGHEST)


def arc_product(source_panel, slots, team_index, team_count):
    arc_length = slots[0].shape[0]
    arc_panel = source_panel
    for power_index in range(team_count.bit_length() - 1):
        shifted = shifted_2(arc_panel, "blk", arc_length * (1 << power_index))
        arc_panel = jnp.where(team_index >> power_index & 1 == 1, shifted, arc_panel)
    empty = jnp.zeros(source_panel.shape, jnp.float32)

    def walk(arc_slot, loop_state):
        partial_value, panel_now = loop_state
        partial_value = partial_value + slot_term(panel_now, arc_slot, slots)
        panel_now = shifted_2(panel_now, "blk", 1)
        return (partial_value, panel_now)

    partial_value, panel_now = lax.fori_loop(0, arc_length - 1, walk, (empty, arc_panel))
    return partial_value + slot_term(panel_now, arc_length - 1, slots)


def per_device(embeddings, degrees, tile_values, tile_rows, tile_columns, slot_counts):
    tile_size = tile_values.shape[-1]
    width_count = embeddings.shape[1]
    block_count = embeddings.shape[0] // tile_size
    slots = (tile_values[0, 0], tile_rows[0, 0], tile_columns[0, 0], slot_counts[0, 0])
    team_index = lax.axis_index("rep")
    team_count = lax.axis_size("rep")
    share_rows = embeddings.shape[0] // team_count
    norm_scale = lax.rsqrt(degrees.astype(jnp.float32))
    current = embeddings
    combined = lax.dynamic_slice_in_dim(embeddings, team_index * share_rows, share_rows)
    for layer_index in range(LAYERS):
        source_panel = (current * norm_scale[:, None]).reshape(block_count, tile_size, width_count)
        partial_value = arc_product(source_panel, slots, team_index, team_count)
        partial_value = partial_value.reshape(block_count * tile_size, width_count)
        current = lax.psum(partial_value, "rep") * norm_scale[:, None]
        combined = combined + lax.dynamic_slice_in_dim(current, team_index * share_rows, share_rows)
    return combined / (LAYERS + 1.0)


def team_kernel(
    teams, chunks, emb_hbm, deg_hbm, tiles_hbm, rows_hbm, cols_hbm, counts_hbm, out_ref,
    emb_own, norm_own, deg_own, tiles, running, running_hi, running_lo,
    rows_ref, cols_ref, counts_ref, keys, a_hi, a_lo,
    x_send, x_recv, x_pair, pair_send, pair_recv, mine, cross_send, cross_recv,
    local_sems, x_send_sems, x_recv_sems, pair_send_sems, pair_recv_sems,
    cross_send_sems, cross_recv_sems,
):
    z = lax.axis_index("blk")
    r = lax.axis_index("rep")
    chip, core = r // 2, r % 2
    sibling, opposite = 2 * chip + (1 - core), 2 * (1 - chip) + core
    slots, tile_size, width = tiles.shape[0], tiles.shape[1], emb_own.shape[1]
    share = emb_own.shape[0]
    piece = share // chunks
    side = a_hi.shape[0] // tile_size
    blocks_own = share // tile_size

    loads = [
        pltpu.make_async_copy(source, target, local_sems.at[i])
        for i, (source, target) in enumerate(
            (
                (deg_hbm.at[pl.ds(r * blocks_own, blocks_own)], deg_own),
                (emb_hbm.at[pl.ds(pl.multiple_of(r * share, share), share)], emb_own),
                (rows_hbm, rows_ref),
                (cols_hbm, cols_ref),
                (counts_hbm, counts_ref),
                (tiles_hbm, tiles),
            )
        )
    ]
    for load in loads:
        load.start()

    barrier = pltpu.get_barrier_semaphore()

    def greet(shard, team):
        pl.semaphore_signal(
            barrier,
            inc=1,
            device_id={"blk": lax.rem(shard, teams), "rep": lax.rem(team, teams)},
            device_id_type=MESH,
        )

    for step in range(1, teams):
        greet(z + step, jnp.int32(step))
        greet(z, r + step)

    @pl.when(r != 0)
    def _():
        for quarter in range(teams):
            greet(z + teams - r, jnp.int32(quarter))

    loads[0].wait()
    for i in range(blocks_own):
        scale_row = lax.rsqrt(deg_own[i].astype(jnp.float32))
        norm_own[i * tile_size : (i + 1) * tile_size] = jnp.broadcast_to(
            scale_row, (width, tile_size)
        ).T
    loads[1].wait()
    x_send[0] = emb_own[...] * norm_own[...]

    @pl.when(r == 0)
    def _():
        pl.semaphore_wait(barrier, 2 * (teams - 1))

    @pl.when(r != 0)
    def _():
        pl.semaphore_wait(barrier, 3 * teams - 2)

    def x_copy(layer, chunk, team):
        rows = pl.ds(chunk * piece, piece)
        return pltpu.make_async_remote_copy(
            src_ref=x_send.at[layer, rows],
            dst_ref=x_recv.at[layer, r, rows],
            send_sem=x_send_sems.at[layer, chunk, team],
            recv_sem=x_recv_sems.at[layer, chunk, r],
            device_id={"blk": lax.rem(z + team, teams), "rep": team},
            device_id_type=MESH,
        )

    def x_arrival(layer, chunk, quarter):
        rows = pl.ds(chunk * piece, piece)
        return pltpu.make_async_remote_copy(
            src_ref=x_send.at[layer, rows],
            dst_ref=x_recv.at[layer, quarter, rows],
            send_sem=x_send_sems.at[layer, chunk, quarter],
            recv_sem=x_recv_sems.at[layer, chunk, quarter],
            device_id={"blk": lax.rem(z + 1, teams), "rep": r},
            device_id_type=MESH,
        )

    def send_x(layer, chunk):
        for team in (2, 3, 1):
            x_copy(layer, chunk, team).start()

        @pl.when(r != 0)
        def _():
            x_copy(layer, chunk, 0).start()

        @pl.when(r == 0)
        def _():
            rows = pl.ds(chunk * piece, piece)
            x_recv[layer, 0, rows] = x_send[layer, rows]

    def take_x(layer):
        for chunk in range(chunks):
            for quarter in range(teams):
                if quarter == 0:
                    @pl.when(r != 0)
                    def _():
                        x_arrival(layer, chunk, 0).wait_recv()
                else:
                    x_arrival(layer, chunk, quarter).wait_recv()
                value = x_recv[layer, quarter, pl.ds(chunk * piece, piece)]
                high = value.astype(jnp.bfloat16)
                low = (value - high.astype(jnp.float32)).astype(jnp.bfloat16)
                first = quarter * share + chunk * piece
                x_pair[first : first + piece, :width] = high
                x_pair[first : first + piece, width:] = low

    def build():
        for load in loads[2:5]:
            load.wait()
        live = counts_ref[0, 0, 0]
        for j in range(slots):
            keys[j] = jnp.where(j < live, rows_ref[j] * side + cols_ref[j], side * side)
        running[0] = jnp.zeros((tile_size, tile_size), jnp.float32)
        running_hi[0] = jnp.zeros((tile_size, tile_size), jnp.bfloat16)
        running_lo[0] = jnp.zeros((tile_size, tile_size), jnp.bfloat16)
        loads[5].wait()

        def accumulate(j, carry):
            own_key = keys[j]
            before = jnp.int32(0)
            for i in range(slots):
                before = jnp.where((keys[i] == own_key) & (i < j), i + 1, before)
            total = running[before] + tiles[j].astype(jnp.float32)
            high = total.astype(jnp.bfloat16)
            running[j + 1] = total
            running_hi[j + 1] = high
            running_lo[j + 1] = (total - high.astype(jnp.float32)).astype(jnp.bfloat16)
            return carry

        lax.fori_loop(0, slots, accumulate, 0)

        def place(row, carry):
            start = pl.multiple_of(row * tile_size, tile_size)
            for column in range(side):
                last = jnp.int32(0)
                for j in range(slots):
                    last = jnp.where(keys[j] == row * side + column, j + 1, last)
                span = slice(column * tile_size, (column + 1) * tile_size)
                a_hi[pl.ds(start, tile_size), span] = running_hi[last]
                a_lo[pl.ds(start, tile_size), span] = running_lo[last]
            return carry

        lax.fori_loop(0, side, place, 0)

    def product(part, chunk):
        start = pl.multiple_of(part * share + chunk * piece, piece)
        both = jnp.dot(
            a_hi[pl.ds(start, piece), :], x_pair[...], preferred_element_type=jnp.float32
        )
        rest = jnp.dot(
            a_lo[pl.ds(start, piece), :], x_pair[:, :width], preferred_element_type=jnp.float32
        )
        return both[:, :width] + (both[:, width:] + rest)

    def neighbour_copy(source, target, send_sems, recv_sems, layer, chunk, team):
        return pltpu.make_async_remote_copy(
            src_ref=source.at[layer, chunk],
            dst_ref=target.at[layer, chunk],
            send_sem=send_sems.at[layer, chunk],
            recv_sem=recv_sems.at[layer, chunk],
            device_id={"blk": z, "rep": team},
            device_id_type=MESH,
        )

    def pair_copy(layer, chunk):
        return neighbour_copy(
            pair_send, pair_recv, pair_send_sems, pair_recv_sems, layer, chunk, sibling
        )

    def cross_copy(layer, chunk):
        return neighbour_copy(
            cross_send, cross_recv, cross_send_sems, cross_recv_sems, layer, chunk, opposite
        )

    for chunk in range(chunks):
        send_x(0, chunk)
    build()
    for layer in range(LAYERS):
        take_x(layer)
        for chunk in range(chunks):
            pair_send[layer, chunk, 0] = product(2 * (1 - chip) + (1 - core), chunk)
            pair_send[layer, chunk, 1] = product(sibling, chunk)
            pair_copy(layer, chunk).start()
            mine[chunk, 0] = product(opposite, chunk)
            mine[chunk, 1] = product(r, chunk)
            if chunk > 0:
                pair_copy(layer, chunk - 1).wait_recv()
                cross_send[layer, chunk - 1] = mine[chunk - 1, 0] + pair_recv[layer, chunk - 1, 0]
                cross_copy(layer, chunk - 1).start()
        pair_copy(layer, chunks - 1).wait_recv()
        cross_send[layer, chunks - 1] = mine[chunks - 1, 0] + pair_recv[layer, chunks - 1, 0]
        cross_copy(layer, chunks - 1).start()
        for chunk in range(chunks):
            rows = pl.ds(chunk * piece, piece)
            cross_copy(layer, chunk).wait_recv()
            total = (mine[chunk, 1] + pair_recv[layer, chunk, 1]) + cross_recv[layer, chunk]
            current = total * norm_own[rows]
            if layer < LAYERS - 1:
                x_send[layer + 1, rows] = current * norm_own[rows]
                send_x(layer + 1, chunk)
                emb_own[rows] = emb_own[rows] + current
            else:
                out_ref[rows] = (emb_own[rows] + current) / (LAYERS + 1.0)

    for layer in range(LAYERS):
        for chunk in range(chunks):
            for team in range(1, teams):
                x_copy(layer, chunk, team).wait_send()

            @pl.when(r != 0)
            def _():
                x_copy(layer, chunk, 0).wait_send()

            pair_copy(layer, chunk).wait_send()
            cross_copy(layer, chunk).wait_send()


def per_device_fused(embeddings, degrees, tile_values, tile_rows, tile_columns, slot_counts):
    teams = lax.axis_size("rep")
    chunks = 2
    slots, tile_size = tile_values.shape[3], tile_values.shape[-1]
    nodes, width = embeddings.shape
    share = nodes // teams
    piece = share // chunks
    f32, bf16, i32 = jnp.float32, jnp.bfloat16, jnp.int32
    hbm = pl.BlockSpec(memory_space=pltpu.HBM)
    dma = pltpu.SemaphoreType.DMA
    return pl.pallas_call(
        functools.partial(team_kernel, teams, chunks),
        name="team_propagate",
        out_shape=jax.ShapeDtypeStruct((share, width), f32),
        in_specs=[hbm] * 6,
        out_specs=pl.BlockSpec(memory_space=pltpu.VMEM),
        scratch_shapes=[
            pltpu.VMEM((share, width), f32),
            pltpu.VMEM((share, width), f32),
            pltpu.VMEM((share // tile_size, 1, tile_size), i32),
            pltpu.VMEM((slots, tile_size, tile_size), bf16),
            pltpu.VMEM((slots + 1, tile_size, tile_size), f32),
            pltpu.VMEM((slots + 1, tile_size, tile_size), bf16),
            pltpu.VMEM((slots + 1, tile_size, tile_size), bf16),
            pltpu.SMEM((slots,), i32),
            pltpu.SMEM((slots,), i32),
            pltpu.SMEM((1, 1, 1), i32),
            pltpu.SMEM((slots,), i32),
            pltpu.VMEM((nodes, nodes), bf16),
            pltpu.VMEM((nodes, nodes), bf16),
            pltpu.VMEM((LAYERS, share, width), f32),
            pltpu.VMEM((LAYERS, teams, share, width), f32),
            pltpu.VMEM((nodes, 2 * width), bf16),
            pltpu.VMEM((LAYERS, chunks, 2, piece, width), f32),
            pltpu.VMEM((LAYERS, chunks, 2, piece, width), f32),
            pltpu.VMEM((chunks, 2, piece, width), f32),
            pltpu.VMEM((LAYERS, chunks, piece, width), f32),
            pltpu.VMEM((LAYERS, chunks, piece, width), f32),
            dma((6,)),
            dma((LAYERS, chunks, teams)),
            dma((LAYERS, chunks, teams)),
            dma((LAYERS, chunks)),
            dma((LAYERS, chunks)),
            dma((LAYERS, chunks)),
            dma((LAYERS, chunks)),
        ],
        compiler_params=pltpu.CompilerParams(
            collective_id=0, has_side_effects=True, vmem_limit_bytes=64 * 1024 * 1024
        ),
    )(
        embeddings,
        degrees.reshape(nodes // tile_size, 1, tile_size),
        tile_values.reshape(slots, tile_size, tile_size),
        tile_rows.reshape(slots),
        tile_columns.reshape(slots),
        slot_counts,
    )


def program_for(mesh):
    teams, cycle = mesh.shape["rep"], mesh.shape["blk"]

    def run(embeddings, degrees, tile_values, tile_rows, tile_columns, slot_counts):
        nodes, tile_size = embeddings.shape[0], tile_values.shape[-1]
        fits = (
            teams == 4
            and cycle == 4
            and tile_values.shape[2] == 1
            and nodes % (teams * tile_size) == 0
            and nodes <= 1024
            and embeddings.shape[1] == tile_size == 128
        )
        form = per_device_fused if fits else per_device
        return form(embeddings, degrees, tile_values, tile_rows, tile_columns, slot_counts)

    return run


def solution(mesh):
    in_specs = (
        P(("groups", "blk"), None),
        P(("groups", "blk")),
        P(("groups", "blk"), "rep", None, None, None, None),
        P(("groups", "blk"), "rep", None, None),
        P(("groups", "blk"), "rep", None, None),
        P(("groups", "blk"), "rep", None),
    )
    out_specs = P(("groups", "blk", "rep"), None)
    return jax.shard_map(
        program_for(mesh), mesh=mesh, in_specs=in_specs, out_specs=out_specs, check_vma=False
    )
```

```python
import functools

import jax
import jax.numpy as jnp
from jax import lax
from jax.experimental import pallas as pl
from jax.experimental.pallas import tpu as pltpu
from jax.sharding import PartitionSpec as P

LAYERS = 2
MESH = pl.DeviceIdType.MESH


def shifted_2(shard, axis, by):
    devices = lax.axis_size(axis)
    return lax.ppermute(shard, axis, [(i, (i + by) % devices) for i in range(devices)])


def slot_term(source_panel, arc_slot, slots):
    tile_values, tile_rows, tile_columns, slot_counts = slots
    slot_total = tile_values.shape[1]
    block_total = source_panel.shape[0]
    columns = lax.dynamic_index_in_dim(tile_columns, arc_slot, 0, keepdims=False)
    values = lax.dynamic_index_in_dim(tile_values, arc_slot, 0, keepdims=False)
    row_blocks = lax.dynamic_index_in_dim(tile_rows, arc_slot, 0, keepdims=False)
    live_count = lax.dynamic_index_in_dim(slot_counts, arc_slot, 0, keepdims=False)
    blocks = jnp.take(source_panel, columns, axis=0)
    products = jnp.einsum(
        "jab,jbw->jaw",
        values,
        blocks,
        precision=lax.Precision.HIGHEST,
        preferred_element_type=jnp.float32,
    )
    live_slots = jnp.arange(slot_total, dtype=jnp.int32) < live_count
    placement = (
        (row_blocks[:, None] == jnp.arange(block_total, dtype=jnp.int32)[None, :])
        & live_slots[:, None]
    ).astype(jnp.float32)
    return jnp.einsum("jc,jaw->caw", placement, products, precision=lax.Precision.HIGHEST)


def arc_product(source_panel, slots, team_index, team_count):
    arc_length = slots[0].shape[0]
    arc_panel = source_panel
    for power_index in range(team_count.bit_length() - 1):
        shifted = shifted_2(arc_panel, "blk", arc_length * (1 << power_index))
        arc_panel = jnp.where(team_index >> power_index & 1 == 1, shifted, arc_panel)
    empty = jnp.zeros(source_panel.shape, jnp.float32)

    def walk(arc_slot, loop_state):
        partial_value, panel_now = loop_state
        partial_value = partial_value + slot_term(panel_now, arc_slot, slots)
        panel_now = shifted_2(panel_now, "blk", 1)
        return (partial_value, panel_now)

    partial_value, panel_now = lax.fori_loop(0, arc_length - 1, walk, (empty, arc_panel))
    return partial_value + slot_term(panel_now, arc_length - 1, slots)


def per_device(embeddings, degrees, tile_values, tile_rows, tile_columns, slot_counts):
    tile_size = tile_values.shape[-1]
    width_count = embeddings.shape[1]
    block_count = embeddings.shape[0] // tile_size
    slots = (tile_values[0, 0], tile_rows[0, 0], tile_columns[0, 0], slot_counts[0, 0])
    team_index = lax.axis_index("rep")
    team_count = lax.axis_size("rep")
    share_rows = embeddings.shape[0] // team_count
    norm_scale = lax.rsqrt(degrees.astype(jnp.float32))
    current = embeddings
    combined = lax.dynamic_slice_in_dim(embeddings, team_index * share_rows, share_rows)
    for layer_index in range(LAYERS):
        source_panel = (current * norm_scale[:, None]).reshape(block_count, tile_size, width_count)
        partial_value = arc_product(source_panel, slots, team_index, team_count)
        partial_value = partial_value.reshape(block_count * tile_size, width_count)
        current = lax.psum(partial_value, "rep") * norm_scale[:, None]
        combined = combined + lax.dynamic_slice_in_dim(current, team_index * share_rows, share_rows)
    return combined / (LAYERS + 1.0)


def team_kernel(
    teams, x_chunks, emb_hbm, deg_hbm, tiles_hbm, rows_hbm, cols_hbm, counts_hbm, out_ref,
    emb_own, norm_own, deg_own, tiles, running, running_hi, running_lo,
    rows_ref, cols_ref, counts_ref, keys, a_hi, a_lo,
    x_send, x_recv, x_pair, pair_send, pair_recv, cross_send, cross_recv,
    local_sems, x_send_sems, x_recv_sems, pair_send_sems, pair_recv_sems,
    cross_send_sems, cross_recv_sems,
):
    z = lax.axis_index("blk")
    r = lax.axis_index("rep")
    chip, core = r // 2, r % 2
    sibling, opposite = 2 * chip + (1 - core), 2 * (1 - chip) + core
    slots, tile_size, width = tiles.shape[0], tiles.shape[1], emb_own.shape[1]
    share = emb_own.shape[0]
    x_piece = share // x_chunks
    side = a_hi.shape[0] // tile_size
    blocks_own = share // tile_size

    loads = [
        pltpu.make_async_copy(source, target, local_sems.at[i])
        for i, (source, target) in enumerate(
            (
                (deg_hbm.at[pl.ds(r * blocks_own, blocks_own)], deg_own),
                (emb_hbm.at[pl.ds(pl.multiple_of(r * share, share), share)], emb_own),
                (rows_hbm, rows_ref),
                (cols_hbm, cols_ref),
                (counts_hbm, counts_ref),
                (tiles_hbm, tiles),
            )
        )
    ]
    for load in loads:
        load.start()

    barrier = pltpu.get_barrier_semaphore()

    def greet(shard, team):
        pl.semaphore_signal(
            barrier,
            inc=1,
            device_id={"blk": lax.rem(shard, teams), "rep": lax.rem(team, teams)},
            device_id_type=MESH,
        )

    for step in range(1, teams):
        greet(z + step, jnp.int32(step))
        greet(z, r + step)

    @pl.when(r != 0)
    def _():
        for quarter in range(teams):
            greet(z + teams - r, jnp.int32(quarter))

    loads[0].wait()
    for i in range(blocks_own):
        scale_row = lax.rsqrt(deg_own[i].astype(jnp.float32))
        norm_own[i * tile_size : (i + 1) * tile_size] = jnp.broadcast_to(
            scale_row, (width, tile_size)
        ).T
    loads[1].wait()
    x_send[0] = emb_own[...] * norm_own[...]

    @pl.when(r == 0)
    def _():
        pl.semaphore_wait(barrier, 2 * (teams - 1))

    @pl.when(r != 0)
    def _():
        pl.semaphore_wait(barrier, 3 * teams - 2)

    def x_copy(layer, chunk, team):
        rows = pl.ds(chunk * x_piece, x_piece)
        return pltpu.make_async_remote_copy(
            src_ref=x_send.at[layer, rows],
            dst_ref=x_recv.at[layer, r, rows],
            send_sem=x_send_sems.at[layer, chunk, team],
            recv_sem=x_recv_sems.at[layer, chunk, r],
            device_id={"blk": lax.rem(z + team, teams), "rep": team},
            device_id_type=MESH,
        )

    def x_arrival(layer, chunk, quarter):
        rows = pl.ds(chunk * x_piece, x_piece)
        return pltpu.make_async_remote_copy(
            src_ref=x_send.at[layer, rows],
            dst_ref=x_recv.at[layer, quarter, rows],
            send_sem=x_send_sems.at[layer, chunk, quarter],
            recv_sem=x_recv_sems.at[layer, chunk, quarter],
            device_id={"blk": lax.rem(z + 1, teams), "rep": r},
            device_id_type=MESH,
        )

    def send_x(layer, chunk):
        for team in (2, 3, 1):
            x_copy(layer, chunk, team).start()

        @pl.when(r != 0)
        def _():
            x_copy(layer, chunk, 0).start()

        @pl.when(r == 0)
        def _():
            rows = pl.ds(chunk * x_piece, x_piece)
            x_recv[layer, 0, rows] = x_send[layer, rows]

    def take_x(layer, chunk):
        for quarter in range(teams):
            if quarter == 0:
                @pl.when(r != 0)
                def _():
                    x_arrival(layer, chunk, 0).wait_recv()
            else:
                x_arrival(layer, chunk, quarter).wait_recv()
            value = x_recv[layer, quarter, pl.ds(chunk * x_piece, x_piece)]
            high = value.astype(jnp.bfloat16)
            low = (value - high.astype(jnp.float32)).astype(jnp.bfloat16)
            first = (chunk * teams + quarter) * x_piece
            x_pair[first : first + x_piece, :width] = high
            x_pair[first : first + x_piece, width:] = low

    def build():
        for load in loads[2:5]:
            load.wait()
        live = counts_ref[0, 0, 0]
        for j in range(slots):
            keys[j] = jnp.where(j < live, rows_ref[j] * side + cols_ref[j], side * side)
        running[0] = jnp.zeros((tile_size, tile_size), jnp.float32)
        running_hi[0] = jnp.zeros((tile_size, tile_size), jnp.bfloat16)
        running_lo[0] = jnp.zeros((tile_size, tile_size), jnp.bfloat16)
        loads[5].wait()

        def accumulate(j, carry):
            own_key = keys[j]
            before = jnp.int32(0)
            for i in range(slots):
                before = jnp.where((keys[i] == own_key) & (i < j), i + 1, before)
            total = running[before] + tiles[j].astype(jnp.float32)
            high = total.astype(jnp.bfloat16)
            running[j + 1] = total
            running_hi[j + 1] = high
            running_lo[j + 1] = (total - high.astype(jnp.float32)).astype(jnp.bfloat16)
            return carry

        lax.fori_loop(0, slots, accumulate, 0)

        def place(row, carry):
            start = pl.multiple_of(row * tile_size, tile_size)
            for column in range(side):
                last = jnp.int32(0)
                for j in range(slots):
                    last = jnp.where(keys[j] == row * side + column, j + 1, last)
                span = slice(column * tile_size, (column + 1) * tile_size)
                a_hi[pl.ds(start, tile_size), span] = running_hi[last]
                a_lo[pl.ds(start, tile_size), span] = running_lo[last]
            return carry

        lax.fori_loop(0, side, place, 0)

    def product(part):
        start = pl.multiple_of(part * share, share)
        both = jnp.dot(
            a_hi[pl.ds(start, share), :], x_pair[...], preferred_element_type=jnp.float32
        )
        rest = jnp.dot(
            a_lo[pl.ds(start, share), :], x_pair[:, :width], preferred_element_type=jnp.float32
        )
        return both[:, :width] + (both[:, width:] + rest)

    def neighbour_copy(source, target, send_sems, recv_sems, layer, chunk, team):
        return pltpu.make_async_remote_copy(
            src_ref=source.at[layer, chunk],
            dst_ref=target.at[layer, chunk],
            send_sem=send_sems.at[layer, chunk],
            recv_sem=recv_sems.at[layer, chunk],
            device_id={"blk": z, "rep": team},
            device_id_type=MESH,
        )

    def pair_copy(layer, chunk):
        return neighbour_copy(
            pair_send, pair_recv, pair_send_sems, pair_recv_sems, layer, chunk, sibling
        )

    def cross_copy(layer, chunk):
        return neighbour_copy(
            cross_send, cross_recv, cross_send_sems, cross_recv_sems, layer, chunk, opposite
        )

    for chunk in range(x_chunks):
        send_x(0, chunk)
    build()
    for layer in range(LAYERS):
        for chunk in range(x_chunks):
            take_x(layer, chunk)
        pair_send[layer, 0] = product(2 * (1 - chip) + (1 - core))
        pair_copy(layer, 0).start()
        for_opposite = product(opposite)
        pair_copy(layer, 0).wait_recv()
        cross_send[layer, 0] = for_opposite + pair_recv[layer, 0]
        cross_copy(layer, 0).start()
        pair_send[layer, 1] = product(sibling)
        pair_copy(layer, 1).start()
        total = product(r)
        pair_copy(layer, 1).wait_recv()
        total = total + pair_recv[layer, 1]
        cross_copy(layer, 0).wait_recv()
        current = (total + cross_recv[layer, 0]) * norm_own[...]
        if layer < LAYERS - 1:
            x_send[layer + 1] = current * norm_own[...]
            for chunk in range(x_chunks):
                send_x(layer + 1, chunk)
            emb_own[...] = emb_own[...] + current
        else:
            out_ref[...] = (emb_own[...] + current) / (LAYERS + 1.0)

    for layer in range(LAYERS):
        for chunk in range(x_chunks):
            for team in range(1, teams):
                x_copy(layer, chunk, team).wait_send()

            @pl.when(r != 0)
            def _():
                x_copy(layer, chunk, 0).wait_send()

        pair_copy(layer, 0).wait_send()
        pair_copy(layer, 1).wait_send()
        cross_copy(layer, 0).wait_send()


def per_device_fused(embeddings, degrees, tile_values, tile_rows, tile_columns, slot_counts):
    teams = lax.axis_size("rep")
    x_chunks = 1
    slots, tile_size = tile_values.shape[3], tile_values.shape[-1]
    nodes, width = embeddings.shape
    share = nodes // teams
    f32, bf16, i32 = jnp.float32, jnp.bfloat16, jnp.int32
    hbm = pl.BlockSpec(memory_space=pltpu.HBM)
    dma = pltpu.SemaphoreType.DMA
    return pl.pallas_call(
        functools.partial(team_kernel, teams, x_chunks),
        name="team_propagate",
        out_shape=jax.ShapeDtypeStruct((share, width), f32),
        in_specs=[hbm] * 6,
        out_specs=pl.BlockSpec(memory_space=pltpu.VMEM),
        scratch_shapes=[
            pltpu.VMEM((share, width), f32),
            pltpu.VMEM((share, width), f32),
            pltpu.VMEM((share // tile_size, 1, tile_size), i32),
            pltpu.VMEM((slots, tile_size, tile_size), bf16),
            pltpu.VMEM((slots + 1, tile_size, tile_size), f32),
            pltpu.VMEM((slots + 1, tile_size, tile_size), bf16),
            pltpu.VMEM((slots + 1, tile_size, tile_size), bf16),
            pltpu.SMEM((slots,), i32),
            pltpu.SMEM((slots,), i32),
            pltpu.SMEM((1, 1, 1), i32),
            pltpu.SMEM((slots,), i32),
            pltpu.VMEM((nodes, nodes), bf16),
            pltpu.VMEM((nodes, nodes), bf16),
            pltpu.VMEM((LAYERS, share, width), f32),
            pltpu.VMEM((LAYERS, teams, share, width), f32),
            pltpu.VMEM((nodes, 2 * width), bf16),
            pltpu.VMEM((LAYERS, 2, share, width), f32),
            pltpu.VMEM((LAYERS, 2, share, width), f32),
            pltpu.VMEM((LAYERS, 1, share, width), f32),
            pltpu.VMEM((LAYERS, 1, share, width), f32),
            dma((6,)),
            dma((LAYERS, x_chunks, teams)),
            dma((LAYERS, x_chunks, teams)),
            dma((LAYERS, 2)),
            dma((LAYERS, 2)),
            dma((LAYERS, 1)),
            dma((LAYERS, 1)),
        ],
        compiler_params=pltpu.CompilerParams(
            collective_id=0, has_side_effects=True, vmem_limit_bytes=64 * 1024 * 1024
        ),
    )(
        embeddings,
        degrees.reshape(nodes // tile_size, 1, tile_size),
        tile_values.reshape(slots, tile_size, tile_size),
        tile_rows.reshape(slots),
        tile_columns.reshape(slots),
        slot_counts,
    )


def program_for(mesh):
    teams, cycle = mesh.shape["rep"], mesh.shape["blk"]

    def run(embeddings, degrees, tile_values, tile_rows, tile_columns, slot_counts):
        nodes, tile_size = embeddings.shape[0], tile_values.shape[-1]
        fits = (
            teams == 4
            and cycle == 4
            and tile_values.shape[2] == 1
            and nodes % (teams * tile_size) == 0
            and nodes <= 1024
            and embeddings.shape[1] == tile_size == 128
        )
        form = per_device_fused if fits else per_device
        return form(embeddings, degrees, tile_values, tile_rows, tile_columns, slot_counts)

    return run


def solution(mesh):
    in_specs = (
        P(("groups", "blk"), None),
        P(("groups", "blk")),
        P(("groups", "blk"), "rep", None, None, None, None),
        P(("groups", "blk"), "rep", None, None),
        P(("groups", "blk"), "rep", None, None),
        P(("groups", "blk"), "rep", None),
    )
    out_specs = P(("groups", "blk", "rep"), None)
    return jax.shard_map(
        program_for(mesh), mesh=mesh, in_specs=in_specs, out_specs=out_specs, check_vma=False
    )
```
